256 devices in a mesh: section: 8 (over z), dom: 32 (over x, y, core).
Axes of the slice: x: 4, y: 4, z: 8, core: 2. Of those that a mesh axis runs over, the one named last changes fastest.
Arguments:
- images: bfloat16 [8, 32, 65536], P('section', None, 'dom'), may hold values from -48 to 48
- weights: bfloat16 [16, 1024, 64, 256], P('section', 'dom'), may hold values from -0.625 to 0.625
- bias: bfloat16 [16, 65536], P('section', 'dom'), may hold values from -12 to 12
- pattern: int32 [16, 1024, 4], P('section'), may hold values from 0 to 1023, as said below
- counts: int32 [16, 1024], P('section', 'dom'), may hold values from 2 to 4, as said below
Outputs:
- scores: bfloat16 [8, 32, 65536], P('section', None, 'dom')
The draws below stay inside these ranges and needn't reach their ends.
Inputs may be any that keep to these rules, and one draw needn't show every extreme that they name: `pattern`: A partition is the 32 consecutive column blocks of one neuron partition (and the row blocks of the same numbers). In each layer, slot 0 of every column block names a row block of its own partition; all slots of one partition's column blocks that name a row block of another partition name the same block of that partition, and every other partition is named so by slot 1 of some column block. Only the first counts[l, n] slots of a column block are live. In each layer every partition has a column block with all 4 slots live.
All inputs are finite; a program needn't handle non-finite values.
Results may differ from the reference program's by a relative error of at most 0.02.
Values may be sent and summed in bfloat16 or wider, within the bound.
No kernel may reach another device: no remote copies, remote signals or barrier semaphores. Data moves between devices by JAX's collectives and lax.ppermute only.
A program may use at most 128 MiB of HBM per device.

```python
import jax
import jax.numpy as jnp
from jax import lax

N = 65536
BS = 64
K = 4
IMAGES = 32
NB = 1024
BLOCKS_DEV = 32
LAYERS = 16
MICRO = 8


def draw_pattern(key, part):
    part_count = NB // BLOCKS_DEV
    base = jax.random.fold_in(key, 11)
    key_pick, key_cand, key_turn = jax.random.split(base, 3)
    picked_block = jax.random.randint(key_pick, (LAYERS, part_count, part_count), 0, BLOCKS_DEV)
    candidate = jax.random.randint(key_cand, (LAYERS, part_count, BLOCKS_DEV, K), 0, BLOCKS_DEV + part_count - 1)
    turn = jax.random.randint(key_turn, (LAYERS, part_count, 1, 1), 0, part_count - 1)
    part_ids = jnp.arange(part_count).reshape(1, part_count, 1, 1)
    column_ids = jnp.arange(BLOCKS_DEV).reshape(1, 1, BLOCKS_DEV, 1)
    slot_ids = jnp.arange(K).reshape(1, 1, 1, K)
    is_local = (candidate < BLOCKS_DEV) | (slot_ids == 0)
    offset = candidate - BLOCKS_DEV + 1
    slot_one = (slot_ids == 1) & (column_ids < part_count - 1)
    offset = jnp.where(slot_one, 1 + (column_ids + turn) % (part_count - 1), offset)
    is_local = jnp.where(slot_one, False, is_local)
    offset = jnp.where(is_local, 1, offset)
    peers = (part_ids + offset) % part_count
    peers = jnp.broadcast_to(peers, (LAYERS, part_count, BLOCKS_DEV, K))
    chosen = jnp.take_along_axis(picked_block, peers.reshape(LAYERS, part_count, BLOCKS_DEV * K), axis=2)
    remote = peers * BLOCKS_DEV + chosen.reshape(LAYERS, part_count, BLOCKS_DEV, K)
    local_rows = part_ids * BLOCKS_DEV + candidate % BLOCKS_DEV
    result = jnp.where(is_local, local_rows, remote)
    return result.reshape(LAYERS, NB, K).astype(jnp.int32)


def draw_counts(key, part):
    part_count = NB // BLOCKS_DEV
    base = jax.random.fold_in(key, 23)
    key_count, key_full = jax.random.split(base, 2)
    drawn = jax.random.randint(key_count, (LAYERS, NB), 2, K + 1)
    chosen = jax.random.randint(key_full, (LAYERS, part_count), 0, BLOCKS_DEV)
    column_ids = jnp.arange(NB) % BLOCKS_DEV
    part_ids = jnp.arange(NB) // BLOCKS_DEV
    full_column = column_ids[None, :] == jnp.take(chosen, part_ids, axis=1)
    return jnp.where(full_column, K, drawn).astype(jnp.int32)


def steps_of(stream_key, dims, cuts, smallest, largest):
    gain = 1.0
    for axis_at, blocks in cuts:
        heights = jax.random.uniform(jax.random.fold_in(jax.random.fold_in(stream_key, 6), axis_at), (blocks,), jnp.float32, smallest / len(cuts), largest / len(cuts))
        gain = gain * jnp.repeat(jnp.exp(heights), dims[axis_at] // blocks).reshape((-1,) + (1,) * (len(dims) - 1 - axis_at))
    return gain


def gaussian(key, dims, deviation, reach, cuts=(), dtype=jnp.bfloat16):
    values = deviation * jax.random.normal(key, dims, jnp.float32)
    if cuts:
        values = values * steps_of(key, dims, cuts, -0.22, 0.18)
    return jnp.clip(values, -reach, reach).astype(dtype)


def setup_inputs(seed: int = 0) -> dict:
    splits = jax.random.split(jax.random.key(seed), 6)
    images = gaussian(splits[0], (MICRO, IMAGES, N), 8.0, 48.0, ((0, 8), (2, 32)))
    weights = gaussian(splits[1], (LAYERS, NB, BS, K * BS), (BS * (K + 2) // 4) ** -0.5, 0.625, ((0, 8), (1, 32)))
    bias = gaussian(splits[2], (LAYERS, N), 2.0, 12.0, ((0, 8), (1, 32)))
    pattern = draw_pattern(jax.random.fold_in(splits[5], 71), 0)
    counts = draw_counts(jax.random.fold_in(splits[5], 71), 0)
    return dict(images=images, weights=weights, bias=bias, pattern=pattern, counts=counts)


def reference(images, weights, bias, pattern, counts):
    live_slots = (jnp.arange(K)[None, None, :] < counts[:, :, None]).astype(jnp.float32)

    def run_micro(current):
        image_rows = current.shape[0]

        def layer_step(current, pieces):
            weight_block, bias_row, block_rows, live_row = pieces
            blocks = current.reshape(image_rows, NB, BS).astype(jnp.float32)
            gathered = jnp.take(blocks, block_rows.reshape(-1).astype(jnp.int32), axis=1)
            gathered = gathered.reshape(image_rows, NB, K, BS)
            weight_full = weight_block.astype(jnp.float32).reshape(NB, BS, K, BS) * live_row[:, None, :, None]
            pre_act = jnp.einsum("bnks,noks->bno", gathered, weight_full).reshape(image_rows, NB * BS)
            pre_act = pre_act + bias_row.astype(jnp.float32)[None, :]
            return jnp.clip(pre_act, 0.0, 32.0).astype(jnp.bfloat16), None

        result, _ = lax.scan(layer_step, current, (weights, bias, pattern, live_slots))
        return result

    return lax.map(run_micro, images)
```

```python
import jax
import jax.numpy as jnp
from jax import lax
from jax.experimental import pallas as pl
from jax.experimental.pallas import tpu as pltpu
from jax.sharding import PartitionSpec as P


def tables(bias, pattern, counts, parts, me):
    layers, columns, slots = pattern.shape
    per = columns // parts
    by_part = pattern.reshape(layers, parts, per * slots)
    wanted = jnp.max(jnp.where(by_part // per == me, by_part % per, 0), axis=2)
    own = lax.dynamic_slice_in_dim(pattern, me * per, per, 1)
    owner = own // per
    source = jnp.where(owner == me, own % per, per + owner)
    live = jnp.arange(slots)[None, None, :] < counts[:, :, None]
    source = jnp.where(live, source, per + parts)
    small = jnp.concatenate([source.reshape(layers, per * slots), wanted], axis=1)
    return jnp.concatenate([bias, small.astype(jnp.bfloat16)], axis=1)


def layer_kernel(layer, step, last, table, cur, arrived, bias, weights, *rest):
    if last:
        new, pool, held, sems = rest
    else:
        new, send, pool, held, sems = rest
    blocks, half, lanes = cur.shape
    parts = arrived.shape[0]
    pieces = held.shape[0]
    each = blocks // pieces
    size = lanes // 2
    slots = held.shape[2] // size

    def fetch(g):
        return pltpu.make_async_copy(weights.at[g, step], held.at[g], sems.at[g])

    for g in range(pieces):
        fetch(g).start()
    low = lax.broadcasted_iota(jnp.int32, (half, lanes), 1) < size

    def spread(tile, at):
        t = tile.astype(jnp.float32)
        r = pltpu.roll(t, size, 1)
        pool[at, 0:half, :] = jnp.where(low, t, r).astype(jnp.bfloat16)
        pool[at, half : 2 * half, :] = jnp.where(low, r, t).astype(jnp.bfloat16)

    for b in range(blocks):
        spread(cur[b], b)
    for q in range(parts):
        spread(arrived[q], blocks + q)
    pool[blocks + parts] = jnp.zeros((2 * half, lanes), jnp.bfloat16)
    low2 = lax.broadcasted_iota(jnp.int32, (2 * half, lanes), 1) < size

    def group(g, carry):
        fetch(g).wait()
        for b in range(each):
            n = g * each + b
            pairs = []
            for s in range(0, slots, 2):
                left = pool[table[layer, n * slots + s]]
                right = pool[table[layer, n * slots + s + 1]]
                pairs.append(jnp.where(low2, left, right))
            picked = jnp.concatenate(pairs, axis=1)
            acc = lax.dot_general(
                picked,
                held[g, b * size : (b + 1) * size, :],
                (((1,), (1,)), ((), ())),
                preferred_element_type=jnp.float32,
            )
            tile = jnp.concatenate([acc[0:half], acc[half : 2 * half]], axis=1)
            tile = tile + bias[layer, pl.ds(n, 1), :]
            new[n] = jnp.clip(tile, 0.0, 32.0).astype(jnp.bfloat16)
        return carry

    lax.fori_loop(0, pieces, group, 0)
    if not last:
        for q in range(parts):
            send[q] = new[table[layer + 1, blocks * slots + q]]


def apply_layer(layer, step, last, table, cur, arrived, bias, weights):
    pieces, _, rows, width = weights.shape
    tile = jax.ShapeDtypeStruct(cur.shape, cur.dtype)
    vmem = pl.BlockSpec(memory_space=pltpu.VMEM)
    blocks, half, lanes = cur.shape
    n_out = 1 if last else 2

    def body(*refs):
        layer_kernel(layer, step, last, *refs)

    out = pl.pallas_call(
        body,
        out_shape=[tile] * n_out,
        in_specs=[pl.BlockSpec(memory_space=pltpu.SMEM), vmem, vmem, vmem, pl.BlockSpec(memory_space=pl.ANY)],
        out_specs=[vmem] * n_out,
        scratch_shapes=[
            pltpu.VMEM((blocks + arrived.shape[0] + 1, 2 * half, lanes), jnp.bfloat16),
            pltpu.VMEM((pieces, rows, width), jnp.bfloat16),
            pltpu.SemaphoreType.DMA((pieces,)),
        ],
        name="layer",
    )(table, cur, arrived, bias, weights)
    return out if not last else (out[0], None)


def shards(images, weights, bias, pattern, counts):
    parts = lax.axis_size("dom")
    sections = lax.axis_size("section")
    me = lax.axis_index("dom")
    own_layers, blocks, size, width = weights.shape
    slots = pattern.shape[2]
    total = own_layers * sections
    rows = blocks // sections * size
    table = tables(bias, pattern, counts, parts, me)
    extra = 16
    table = jnp.pad(table, ((0, 0), (0, extra * width - table.shape[1])))
    table = table.reshape(own_layers, 1, extra, width)
    table = jnp.broadcast_to(table, (own_layers, sections, extra, width))
    both = jnp.concatenate([weights.reshape(own_layers, sections, rows, width), table], axis=2)
    scattered = lax.all_to_all(both, "section", split_axis=1, concat_axis=0, tiled=True)
    scattered = scattered.reshape(total, rows + extra, width)
    chunk = 4
    filled = [
        lax.all_gather(scattered[c : c + chunk, :rows], "section", axis=0, tiled=False)
        for c in range(0, total, chunk)
    ]
    flat = scattered[:, rows:].reshape(total, extra * width)
    all_bias = flat[:, : blocks * size].reshape(total, blocks, size).astype(jnp.float32)
    all_bias = jnp.concatenate([all_bias, all_bias], axis=2)
    table = flat[:, blocks * size : blocks * (size + slots) + parts].astype(jnp.int32)

    half = images.shape[1] // 2
    cur = images.reshape(2, half, blocks, size).transpose(2, 1, 0, 3).reshape(blocks, half, 2 * size)
    send = jnp.take(cur, table[0, blocks * slots :], axis=0)
    for layer in range(total):
        arrived = lax.all_to_all(send, "dom", split_axis=0, concat_axis=0, tiled=True)
        cur, send = apply_layer(
            layer, layer % chunk, layer == total - 1, table, cur, arrived, all_bias, filled[layer // chunk]
        )
    out = cur.reshape(blocks, half, 2, size).transpose(2, 1, 0, 3)
    return out.reshape(images.shape)


def solution(mesh):
    placed = (
        P("section", None, "dom"),
        P("section", "dom", None, None),
        P("section", "dom"),
        P("section", None, None),
        P("section", "dom"),
    )
    return jax.shard_map(
        shards, mesh=mesh, in_specs=placed, out_specs=P("section", None, "dom"), check_vma=False
    )
```

```python
import jax
import jax.numpy as jnp
from jax import lax
from jax.experimental import pallas as pl
from jax.experimental.pallas import tpu as pltpu
from jax.sharding import PartitionSpec as P


def tables(bias, pattern, counts, parts, me):
    layers, columns, slots = pattern.shape
    per = columns // parts
    by_part = pattern.reshape(layers, parts, per * slots)
    wanted = jnp.max(jnp.where(by_part // per == me, by_part % per, 0), axis=2)
    own = lax.dynamic_slice_in_dim(pattern, me * per, per, 1)
    owner = own // per
    source = jnp.where(owner == me, own % per, per + owner)
    live = jnp.arange(slots)[None, None, :] < counts[:, :, None]
    source = jnp.where(live, source, per + parts)
    small = jnp.concatenate([source.reshape(layers, per * slots), wanted], axis=1)
    return jnp.concatenate([bias, small.astype(jnp.bfloat16)], axis=1)


def layer_kernel(layer, last, table, cur, arrived, bias, weights, *rest):
    if last:
        new, pool = rest
    else:
        new, send, pool = rest
    blocks, half, lanes = cur.shape
    parts = arrived.shape[0]
    size = lanes // 2
    slots = weights.shape[2] // size
    low = lax.broadcasted_iota(jnp.int32, (half, lanes), 1) < size

    def spread(tile, at):
        t = tile.astype(jnp.float32)
        r = pltpu.roll(t, size, 1)
        pool[at, 0:half, :] = jnp.where(low, t, r).astype(jnp.bfloat16)
        pool[at, half : 2 * half, :] = jnp.where(low, r, t).astype(jnp.bfloat16)

    for b in range(blocks):
        spread(cur[b], b)
    for q in range(parts):
        spread(arrived[q], blocks + q)
    pool[blocks + parts] = jnp.zeros((2 * half, lanes), jnp.bfloat16)
    low2 = lax.broadcasted_iota(jnp.int32, (2 * half, lanes), 1) < size

    def column(n, carry):
        pairs = []
        for s in range(0, slots, 2):
            left = pool[table[layer, n * slots + s]]
            right = pool[table[layer, n * slots + s + 1]]
            pairs.append(jnp.where(low2, left, right))
        acc = lax.dot_general(
            jnp.concatenate(pairs, axis=1),
            weights[n],
            (((1,), (1,)), ((), ())),
            preferred_element_type=jnp.float32,
        )
        tile = jnp.concatenate([acc[0:half], acc[half : 2 * half]], axis=1)
        tile = tile + bias[layer, pl.ds(n, 1), :]
        new[n] = jnp.clip(tile, 0.0, 32.0).astype(jnp.bfloat16)
        return carry

    lax.fori_loop(0, blocks, column, 0, unroll=16)
    if not last:
        for q in range(parts):
            send[q] = new[table[layer + 1, blocks * slots + q]]


def on_chip(x):
    return pltpu.with_memory_space_constraint(x, pltpu.VMEM)


def apply_layer(layer, last, table, cur, arrived, bias, weights):
    tile = pltpu.VMEM(cur.shape, cur.dtype)
    vmem = pl.BlockSpec(memory_space=pltpu.VMEM)
    blocks, half, lanes = cur.shape
    n_out = 1 if last else 2

    def body(*refs):
        layer_kernel(layer, last, *refs)

    out = pl.pallas_call(
        body,
        out_shape=[tile] * n_out,
        in_specs=[pl.BlockSpec(memory_space=pltpu.SMEM), vmem, vmem, vmem, vmem],
        out_specs=[vmem] * n_out,
        scratch_shapes=[
            pltpu.VMEM((blocks + arrived.shape[0] + 1, 2 * half, lanes), jnp.bfloat16),
        ],
        name="layer",
    )(table, on_chip(cur), on_chip(arrived), on_chip(bias), on_chip(weights))
    return out if not last else (out[0], None)


def shards(images, weights, bias, pattern, counts):
    parts = lax.axis_size("dom")
    sections = lax.axis_size("section")
    me = lax.axis_index("dom")
    own_layers, blocks, size, width = weights.shape
    slots = pattern.shape[2]
    total = own_layers * sections
    rows = blocks // sections * size
    table = tables(bias, pattern, counts, parts, me)
    extra = 16
    table = jnp.pad(table, ((0, 0), (0, extra * width - table.shape[1])))
    table = table.reshape(own_layers, 1, extra, width)
    table = jnp.broadcast_to(table, (own_layers, sections, extra, width))
    both = jnp.concatenate([weights.reshape(own_layers, sections, rows, width), table], axis=2)
    scattered = lax.all_to_all(both, "section", split_axis=1, concat_axis=0, tiled=True)
    scattered = scattered.reshape(total, rows + extra, width)
    chunk = 4
    filled = [
        lax.all_gather(scattered[c : c + chunk, :rows], "section", axis=0, tiled=False)
        for c in range(0, total, chunk)
    ]
    flat = scattered[:, rows:].reshape(total, extra * width)
    all_bias = flat[:, : blocks * size].reshape(total, blocks, size).astype(jnp.float32)
    all_bias = jnp.concatenate([all_bias, all_bias], axis=2)
    table = flat[:, blocks * size : blocks * (size + slots) + parts].astype(jnp.int32)

    half = images.shape[1] // 2
    cur = images.reshape(2, half, blocks, size).transpose(2, 1, 0, 3).reshape(blocks, half, 2 * size)
    send = jnp.take(cur, table[0, blocks * slots :], axis=0)
    for layer in range(total):
        arrived = lax.all_to_all(send, "dom", split_axis=0, concat_axis=0, tiled=True)
        held = filled[layer // chunk][:, layer % chunk].reshape(blocks, size, width)
        cur, send = apply_layer(layer, layer == total - 1, table, cur, arrived, all_bias, held)
    out = cur.reshape(blocks, half, 2, size).transpose(2, 1, 0, 3)
    return out.reshape(images.shape)


def solution(mesh):
    placed = (
        P("section", None, "dom"),
        P("section", "dom", None, None),
        P("section", "dom"),
        P("section", None, None),
        P("section", "dom"),
    )
    return jax.shard_map(
        shards, mesh=mesh, in_specs=placed, out_specs=P("section", None, "dom"), check_vma=False
    )
```

```python
import jax
import jax.numpy as jnp
from jax import lax
from jax.experimental import pallas as pl
from jax.experimental.pallas import tpu as pltpu
from jax.sharding import PartitionSpec as P


def tables(bias, pattern, counts, parts, me):
    layers, columns, slots = pattern.shape
    per = columns // parts
    by_part = pattern.reshape(layers, parts, per * slots)
    wanted = jnp.max(jnp.where(by_part // per == me, by_part % per, 0), axis=2)
    own = lax.dynamic_slice_in_dim(pattern, me * per, per, 1)
    owner = own // per
    source = jnp.where(owner == me, own % per, per + owner)
    live = jnp.arange(slots)[None, None, :] < counts[:, :, None]
    source = jnp.where(live, source, per + parts)
    small = jnp.concatenate([source.reshape(layers, per * slots), wanted], axis=1)
    return jnp.concatenate([bias, small.astype(jnp.bfloat16)], axis=1)


def layer_kernel(layer, step, last, table, cur, arrived, bias, weights, *rest):
    if last:
        new, pool = rest
    else:
        new, send, pool = rest
    blocks, half, lanes = cur.shape
    parts = arrived.shape[0]
    size = lanes // 2
    slots = weights.shape[3] // size
    each = blocks // weights.shape[0]
    low = lax.broadcasted_iota(jnp.int32, (half, lanes), 1) < size

    def spread(tile, at):
        t = tile.astype(jnp.float32)
        r = pltpu.roll(t, size, 1)
        pool[at, 0:half, :] = jnp.where(low, t, r).astype(jnp.bfloat16)
        pool[at, half : 2 * half, :] = jnp.where(low, r, t).astype(jnp.bfloat16)

    for b in range(blocks):
        spread(cur[b], b)
    for q in range(parts):
        spread(arrived[q], blocks + q)
    pool[blocks + parts] = jnp.zeros((2 * half, lanes), jnp.bfloat16)
    low2 = lax.broadcasted_iota(jnp.int32, (2 * half, lanes), 1) < size

    def column(n, carry):
        pairs = []
        for s in range(0, slots, 2):
            left = pool[table[layer, n * slots + s]]
            right = pool[table[layer, n * slots + s + 1]]
            pairs.append(jnp.where(low2, left, right))
        acc = lax.dot_general(
            jnp.concatenate(pairs, axis=1),
            weights[n // each, step, pl.ds(pl.multiple_of(n % each * size, size), size), :],
            (((1,), (1,)), ((), ())),
            preferred_element_type=jnp.float32,
        )
        tile = jnp.concatenate([acc[0:half], acc[half : 2 * half]], axis=1)
        tile = tile + bias[layer, pl.ds(n, 1), :]
        new[n] = jnp.clip(tile, 0.0, 32.0).astype(jnp.bfloat16)
        return carry

    lax.fori_loop(0, blocks, column, 0, unroll=16)
    if not last:
        for q in range(parts):
            send[q] = new[table[layer + 1, blocks * slots + q]]


def on_chip(x):
    return pltpu.with_memory_space_constraint(x, pltpu.VMEM)


def apply_layer(layer, step, last, table, cur, arrived, bias, weights):
    tile = pltpu.VMEM(cur.shape, cur.dtype)
    vmem = pl.BlockSpec(memory_space=pltpu.VMEM)
    blocks, half, lanes = cur.shape
    n_out = 1 if last else 2

    def body(*refs):
        layer_kernel(layer, step, last, *refs)

    out = pl.pallas_call(
        body,
        out_shape=[tile] * n_out,
        in_specs=[pl.BlockSpec(memory_space=pltpu.SMEM), vmem, vmem, vmem, vmem],
        out_specs=[vmem] * n_out,
        scratch_shapes=[
            pltpu.VMEM((blocks + arrived.shape[0] + 1, 2 * half, lanes), jnp.bfloat16),
        ],
        compiler_params=pltpu.CompilerParams(vmem_limit_bytes=4 * 1024 * 1024),
        name="layer",
    )(table, on_chip(cur), on_chip(arrived), on_chip(bias), on_chip(weights))
    return out if not last else (out[0], None)


def shards(images, weights, bias, pattern, counts):
    parts = lax.axis_size("dom")
    sections = lax.axis_size("section")
    me = lax.axis_index("dom")
    own_layers, blocks, size, width = weights.shape
    slots = pattern.shape[2]
    total = own_layers * sections
    rows = blocks // sections * size
    table = tables(bias, pattern, counts, parts, me)
    flat = lax.all_gather(jnp.pad(table, ((0, 0), (0, -table.shape[1] % 1024))), "section", axis=0, tiled=True)
    split = weights.reshape(own_layers, sections, rows, width)
    scattered = lax.all_to_all(split, "section", split_axis=1, concat_axis=0, tiled=True)
    scattered = scattered.reshape(total, rows, width)
    chunk = 4
    filled = [
        lax.all_gather(scattered[c : c + chunk], "section", axis=0, tiled=False)
        for c in range(0, total, chunk)
    ]
    all_bias = flat[:, : blocks * size].reshape(total, blocks, size).astype(jnp.float32)
    all_bias = jnp.concatenate([all_bias, all_bias], axis=2)
    table = flat[:, blocks * size : blocks * (size + slots) + parts].astype(jnp.int32)

    half = images.shape[1] // 2
    cur = images.reshape(2, half, blocks, size).transpose(2, 1, 0, 3).reshape(blocks, half, 2 * size)
    send = jnp.take(cur, table[0, blocks * slots :], axis=0)
    for layer in range(total):
        arrived = lax.all_to_all(send, "dom", split_axis=0, concat_axis=0, tiled=True)
        cur, send = apply_layer(
            layer, layer % chunk, layer == total - 1, table, cur, arrived, all_bias, filled[layer // chunk]
        )
    out = cur.reshape(blocks, half, 2, size).transpose(2, 1, 0, 3)
    return out.reshape(images.shape)


def solution(mesh):
    placed = (
        P("section", None, "dom"),
        P("section", "dom", None, None),
        P("section", "dom"),
        P("section", None, None),
        P("section", "dom"),
    )
    return jax.shard_map(
        shards, mesh=mesh, in_specs=placed, out_specs=P("section", None, "dom"), check_vma=False
    )
```

```python
import jax
import jax.numpy as jnp
from jax import lax
from jax.experimental import pallas as pl
from jax.experimental.pallas import tpu as pltpu
from jax.sharding import PartitionSpec as P


def tables(bias, pattern, counts, parts, me):
    layers, columns, slots = pattern.shape
    per = columns // parts
    by_part = pattern.reshape(layers, parts, per * slots)
    wanted = jnp.max(jnp.where(by_part // per == me, by_part % per, 0), axis=2)
    own = lax.dynamic_slice_in_dim(pattern, me * per, per, 1)
    owner = own // per
    source = jnp.where(owner == me, own % per, per + owner)
    live = jnp.arange(slots)[None, None, :] < counts[:, :, None]
    source = jnp.where(live, source, per + parts)
    small = jnp.concatenate([source.reshape(layers, per * slots), wanted], axis=1)
    return jnp.concatenate([bias, small.astype(jnp.bfloat16)], axis=1)


def layer_kernel(layer, step, follow, unroll, table, cur, arrived, bias, weights, *rest):
    if follow is None:
        new, pool = rest
    else:
        new, send, pool = rest
    blocks, half, lanes = cur.shape
    parts = arrived.shape[0]
    size = lanes // 2
    slots = weights.shape[2] // size
    each = blocks // weights.shape[0]
    base = step * each * size
    low = lax.broadcasted_iota(jnp.int32, (half, lanes), 1) < size

    def spread(tile, at):
        t = tile.astype(jnp.float32)
        r = pltpu.roll(t, size, 1)
        pool[at, 0:half, :] = jnp.where(low, t, r).astype(jnp.bfloat16)
        pool[at, half : 2 * half, :] = jnp.where(low, r, t).astype(jnp.bfloat16)

    for b in range(blocks):
        spread(cur[b], b)
    for q in range(parts):
        spread(arrived[q], blocks + q)
    pool[blocks + parts] = jnp.zeros((2 * half, lanes), jnp.bfloat16)
    low2 = lax.broadcasted_iota(jnp.int32, (2 * half, lanes), 1) < size

    def column(n, carry):
        pairs = []
        for s in range(0, slots, 2):
            left = pool[table[layer, n * slots + s]]
            right = pool[table[layer, n * slots + s + 1]]
            pairs.append(jnp.where(low2, left, right))
        acc = lax.dot_general(
            jnp.concatenate(pairs, axis=1),
            weights[n // each, pl.ds(pl.multiple_of(base + n % each * size, size), size), :],
            (((1,), (1,)), ((), ())),
            preferred_element_type=jnp.float32,
        )
        tile = jnp.concatenate([acc[0:half], acc[half : 2 * half]], axis=1)
        tile = tile + bias[layer, pl.ds(n, 1), :]
        new[n] = jnp.clip(tile, 0.0, 32.0).astype(jnp.bfloat16)
        return carry

    lax.fori_loop(0, blocks, column, 0, unroll=unroll)
    if follow is not None:
        for q in range(parts):
            send[q] = new[table[follow, blocks * slots + q]]


def on_chip(x):
    return pltpu.with_memory_space_constraint(x, pltpu.VMEM)


def apply_layer(layer, step, follow, unroll, table, cur, arrived, bias, weights):
    tile = pltpu.VMEM(cur.shape, cur.dtype)
    vmem = pl.BlockSpec(memory_space=pltpu.VMEM)
    blocks, half, lanes = cur.shape
    n_out = 1 if follow is None else 2

    def body(*refs):
        layer_kernel(layer, step, follow, unroll, *refs)

    out = pl.pallas_call(
        body,
        out_shape=[tile] * n_out,
        in_specs=[pl.BlockSpec(memory_space=pltpu.SMEM), vmem, vmem, vmem, vmem],
        out_specs=[vmem] * n_out,
        scratch_shapes=[
            pltpu.VMEM((blocks + arrived.shape[0] + 1, 2 * half, lanes), jnp.bfloat16),
        ],
        compiler_params=pltpu.CompilerParams(vmem_limit_bytes=(3 + half // 16) * 1024 * 1024),
        name="layer",
    )(table, on_chip(cur), on_chip(arrived), on_chip(bias), on_chip(weights))
    return out if follow is not None else (out[0], None)


def split_table(flat, blocks, size, slots, parts):
    rows = flat.shape[0]
    bias = flat[:, : blocks * size].reshape(rows, blocks, size).astype(jnp.float32)
    words = flat[:, blocks * size : blocks * (size + slots) + parts].astype(jnp.int32)
    return jnp.concatenate([bias, bias], axis=2), words


def exchange(send):
    return lax.all_to_all(send, "dom", split_axis=0, concat_axis=0, tiled=True)


def place_kernel(here, *refs):
    count = len(refs) - 4
    pieces, held, stage, take, give = refs[:count], *refs[count:]
    sources = [lax.rem(here[0] + count - d, count) for d in range(count)]
    ins = [pltpu.make_async_copy(pieces[d], stage.at[d], take.at[d]) for d in range(count)]
    outs = [pltpu.make_async_copy(stage.at[d], held.at[sources[d]], give.at[d]) for d in range(count)]
    for copy in ins:
        copy.start()
    for copy, onward in zip(ins, outs):
        copy.wait()
        onward.start()
    for onward in outs:
        onward.wait()


def place(here, pieces):
    count = len(pieces)
    shape = (count, *pieces[0].shape)
    hbm = pl.BlockSpec(memory_space=pl.ANY)
    return pl.pallas_call(
        place_kernel,
        out_shape=jax.ShapeDtypeStruct(shape, pieces[0].dtype),
        in_specs=[pl.BlockSpec(memory_space=pltpu.SMEM)] + [hbm] * count,
        out_specs=hbm,
        scratch_shapes=[
            pltpu.VMEM(shape, pieces[0].dtype),
            pltpu.SemaphoreType.DMA((count,)),
            pltpu.SemaphoreType.DMA((count,)),
        ],
        compiler_params=pltpu.CompilerParams(vmem_limit_bytes=4 * 1024 * 1024),
        name="place",
    )(here.reshape(1), *pieces)


def shards(images, weights, bias, pattern, counts):
    parts = lax.axis_size("dom")
    sections = lax.axis_size("section")
    me = lax.axis_index("dom")
    here = lax.axis_index("section")
    own_layers, blocks, size, width = weights.shape
    slots = pattern.shape[2]
    total = own_layers * sections
    rows = blocks // sections * size
    half = images.shape[1] // 2
    words = blocks * slots
    pair = [(0, 1), (1, 0)]
    early = 2 * own_layers
    even = here % 2 == 0

    cur = images.reshape(2, half, blocks, size).transpose(2, 1, 0, 3).reshape(blocks, half, 2 * size)
    shares = [cur]
    for k in range(1, sections // 2):
        shares.append(lax.ppermute(cur, "section", [(2 * k, 0), (2 * k + 1, 1)]))
    table = tables(bias, pattern, counts, parts, me)
    table = jnp.pad(table, ((0, 0), (0, -table.shape[1] % 1024)))
    other = lax.ppermute(table, "section", pair)
    partner = []
    for k in range(own_layers):
        partner.append(lax.ppermute(weights[k], "section", pair))

    split = weights.reshape(own_layers, sections, rows, width)
    pieces = [lax.dynamic_index_in_dim(split, here, 1, keepdims=False)]
    for d in range(1, sections):
        piece = lax.dynamic_index_in_dim(split, (here + d) % sections, 1, keepdims=False)
        pairs = [(s, (s + d) % sections) for s in range(2, sections)]
        pieces.append(lax.ppermute(piece, "section", pairs))
    both = jnp.concatenate([jnp.where(even, table, other), jnp.where(even, other, table)], axis=0)
    pair_bias, pair_words = split_table(both, blocks, size, slots, parts)

    def mine(layer):
        k = layer % own_layers
        ours = even if layer < own_layers else jnp.logical_not(even)
        return jnp.where(ours, weights[k], partner[k]).reshape(1, blocks * size, width)


    cur = jnp.concatenate(shares, axis=1)
    send = jnp.take(cur, pair_words[0, words:], axis=0)
    chunk = 4
    for layer in range(early):
        arrived = exchange(send)
        if layer == 1:
            arrived, pieces, partner[1] = lax.optimization_barrier((arrived, pieces, partner[1]))
            held = place(here, pieces).reshape(total * rows, width)
            filled = {}
            for c in range(early, total, chunk):
                part = held[c * rows : (c + chunk) * rows]
                if c == early:
                    lines = table.reshape(-1, width)
                    lines = jnp.pad(lines, ((0, -lines.shape[0] % 16), (0, 0)))
                    part = jnp.concatenate([part, lines], axis=0)
                filled[c] = lax.all_gather(part, "section", axis=0, tiled=False)
        follow = layer + 1 if layer + 1 < early else None
        cur, send = apply_layer(layer, 0, follow, 4, pair_words, cur, arrived, pair_bias, mine(layer))

    ready = cur.reshape(blocks, sections // 2, half, 2 * size)
    back = jnp.zeros_like(ready[:, 0])
    for k in range(1, sections // 2):
        back = back + lax.ppermute(ready[:, k], "section", [(0, 2 * k), (1, 2 * k + 1)])
    cur = jnp.where(here < 2, ready[:, 0], back)

    flat = filled[early][:, chunk * rows : chunk * rows + table.size // width].reshape(total, -1)
    all_bias, table = split_table(flat, blocks, size, slots, parts)
    send = jnp.take(cur, table[early, words:], axis=0)
    for layer in range(early, total):
        step = (layer - early) % chunk
        follow = layer + 1 if layer + 1 < total else None
        cur, send = apply_layer(
            layer, step, follow, 16, table, cur, exchange(send), all_bias, filled[layer - step]
        )
    out = cur.reshape(blocks, half, 2, size).transpose(2, 1, 0, 3)
    return out.reshape(images.shape)


def solution(mesh):
    placed = (
        P("section", None, "dom"),
        P("section", "dom", None, None),
        P("section", "dom"),
        P("section", None, None),
        P("section", "dom"),
    )
    return jax.shard_map(
        shards, mesh=mesh, in_specs=placed, out_specs=P("section", None, "dom"), check_vma=False
    )
```

```python
import jax
import jax.numpy as jnp
from jax import lax
from jax.experimental import pallas as pl
from jax.experimental.pallas import tpu as pltpu
from jax.sharding import PartitionSpec as P


def tables(bias, pattern, counts, parts, me):
    layers, columns, slots = pattern.shape
    per = columns // parts
    by_part = pattern.reshape(layers, parts, per * slots)
    wanted = jnp.max(jnp.where(by_part // per == me, by_part % per, 0), axis=2)
    own = lax.dynamic_slice_in_dim(pattern, me * per, per, 1)
    owner = own // per
    source = jnp.where(owner == me, own % per, per + owner)
    live = jnp.arange(slots)[None, None, :] < counts[:, :, None]
    source = jnp.where(live, source, per + parts)
    small = jnp.concatenate([source.reshape(layers, per * slots), wanted], axis=1)
    return jnp.concatenate([bias, small.astype(jnp.bfloat16)], axis=1)


def layer_kernel(layer, step, follow, unroll, table, cur, arrived, bias, weights, *rest):
    if follow is None:
        new, pool = rest
    else:
        new, send, pool = rest
    blocks, half, lanes = cur.shape
    parts = arrived.shape[0]
    size = lanes // 2
    slots = weights.shape[2] // size
    each = blocks // weights.shape[0]
    base = step * each * size
    low = lax.broadcasted_iota(jnp.int32, (half, lanes), 1) < size

    def spread(tile, at):
        t = tile.astype(jnp.float32)
        r = pltpu.roll(t, size, 1)
        pool[at, 0:half, :] = jnp.where(low, t, r).astype(jnp.bfloat16)
        pool[at, half : 2 * half, :] = jnp.where(low, r, t).astype(jnp.bfloat16)

    for b in range(blocks):
        spread(cur[b], b)
    for q in range(parts):
        spread(arrived[q], blocks + q)
    pool[blocks + parts] = jnp.zeros((2 * half, lanes), jnp.bfloat16)
    low2 = lax.broadcasted_iota(jnp.int32, (2 * half, lanes), 1) < size

    def column(n, carry):
        pairs = []
        for s in range(0, slots, 2):
            left = pool[table[layer, n * slots + s]]
            right = pool[table[layer, n * slots + s + 1]]
            pairs.append(jnp.where(low2, left, right))
        acc = lax.dot_general(
            jnp.concatenate(pairs, axis=1),
            weights[n // each, pl.ds(pl.multiple_of(base + n % each * size, size), size), :],
            (((1,), (1,)), ((), ())),
            preferred_element_type=jnp.float32,
        )
        tile = jnp.concatenate([acc[0:half], acc[half : 2 * half]], axis=1)
        tile = tile + bias[layer, pl.ds(n, 1), :]
        new[n] = jnp.clip(tile, 0.0, 32.0).astype(jnp.bfloat16)
        return carry

    lax.fori_loop(0, blocks, column, 0, unroll=unroll)
    if follow is not None:
        for q in range(parts):
            send[q] = new[table[follow, blocks * slots + q]]


def on_chip(x):
    return pltpu.with_memory_space_constraint(x, pltpu.VMEM)


def apply_layer(layer, step, follow, unroll, table, cur, arrived, bias, weights):
    tile = pltpu.VMEM(cur.shape, cur.dtype)
    vmem = pl.BlockSpec(memory_space=pltpu.VMEM)
    blocks, half, lanes = cur.shape
    n_out = 1 if follow is None else 2

    def body(*refs):
        layer_kernel(layer, step, follow, unroll, *refs)

    out = pl.pallas_call(
        body,
        out_shape=[tile] * n_out,
        in_specs=[pl.BlockSpec(memory_space=pltpu.SMEM), vmem, vmem, vmem, vmem],
        out_specs=[vmem] * n_out,
        scratch_shapes=[
            pltpu.VMEM((blocks + arrived.shape[0] + 1, 2 * half, lanes), jnp.bfloat16),
        ],
        compiler_params=pltpu.CompilerParams(vmem_limit_bytes=(3 + half // 16) * 1024 * 1024),
        name="layer",
    )(table, on_chip(cur), on_chip(arrived), on_chip(bias), on_chip(weights))
    return out if follow is not None else (out[0], None)


def split_table(flat, blocks, size, slots, parts):
    rows = flat.shape[0]
    bias = flat[:, : blocks * size].reshape(rows, blocks, size).astype(jnp.float32)
    words = flat[:, blocks * size : blocks * (size + slots) + parts].astype(jnp.int32)
    return jnp.concatenate([bias, bias], axis=2), words


def exchange(send):
    return lax.all_to_all(send, "dom", split_axis=0, concat_axis=0, tiled=True)


def place_kernel(here, *refs):
    count = len(refs) - 4
    pieces, held, stage, take, give = refs[:count], *refs[count:]
    sources = [lax.rem(here[0] + count - d, count) for d in range(count)]
    ins = [pltpu.make_async_copy(pieces[d], stage.at[d], take.at[d]) for d in range(count)]
    outs = [pltpu.make_async_copy(stage.at[d], held.at[sources[d]], give.at[d]) for d in range(count)]
    for copy in ins:
        copy.start()
    for copy, onward in zip(ins, outs):
        copy.wait()
        onward.start()
    for onward in outs:
        onward.wait()


def place(here, pieces):
    count = len(pieces)
    shape = (count, *pieces[0].shape)
    hbm = pl.BlockSpec(memory_space=pl.ANY)
    return pl.pallas_call(
        place_kernel,
        out_shape=jax.ShapeDtypeStruct(shape, pieces[0].dtype),
        in_specs=[pl.BlockSpec(memory_space=pltpu.SMEM)] + [hbm] * count,
        out_specs=hbm,
        scratch_shapes=[
            pltpu.VMEM(shape, pieces[0].dtype),
            pltpu.SemaphoreType.DMA((count,)),
            pltpu.SemaphoreType.DMA((count,)),
        ],
        compiler_params=pltpu.CompilerParams(vmem_limit_bytes=4 * 1024 * 1024),
        name="place",
    )(here.reshape(1), *pieces)


def shards(images, weights, bias, pattern, counts):
    parts = lax.axis_size("dom")
    sections = lax.axis_size("section")
    me = lax.axis_index("dom")
    here = lax.axis_index("section")
    own_layers, blocks, size, width = weights.shape
    slots = pattern.shape[2]
    total = own_layers * sections
    rows = blocks // sections * size
    half = images.shape[1] // 2
    words = blocks * slots
    pair = [(0, 1), (1, 0)]
    early = 2 * own_layers
    even = here % 2 == 0

    cur = images.reshape(2, half, blocks, size).transpose(2, 1, 0, 3).reshape(blocks, half, 2 * size)
    shares = [cur]
    for k in range(1, sections // 2):
        shares.append(lax.ppermute(cur, "section", [(2 * k, 0), (2 * k + 1, 1)]))
    table = tables(bias, pattern, counts, parts, me)
    table = jnp.pad(table, ((0, 0), (0, -table.shape[1] % 1024)))
    other = lax.ppermute(table, "section", pair)
    partner = []
    for k in range(own_layers):
        partner.append(lax.ppermute(weights[k], "section", pair))

    split = weights.reshape(own_layers, sections, rows, width)
    pieces = [lax.dynamic_index_in_dim(split, here, 1, keepdims=False)]
    for d in range(1, sections):
        piece = lax.dynamic_index_in_dim(split, (here + d) % sections, 1, keepdims=False)
        pairs = [(s, (s + d) % sections) for s in range(2, sections)]
        pieces.append(lax.ppermute(piece, "section", pairs))
    both = jnp.concatenate([jnp.where(even, table, other), jnp.where(even, other, table)], axis=0)
    pair_bias, pair_words = split_table(both, blocks, size, slots, parts)

    def mine(layer):
        k = layer % own_layers
        ours = even if layer < own_layers else jnp.logical_not(even)
        return jnp.where(ours, weights[k], partner[k]).reshape(1, blocks * size, width)


    cur = jnp.concatenate(shares, axis=1)
    send = jnp.take(cur, pair_words[0, words:], axis=0)
    edges = [early, 7, 11, 15, total]
    for layer in range(early):
        arrived = exchange(send)
        if layer == 1:
            arrived, pieces, partner[1] = lax.optimization_barrier((arrived, pieces, partner[1]))
            held = place(here, pieces).reshape(total * rows, width)
            lines = table.reshape(-1, width)
            lines = jnp.pad(lines, ((0, -lines.shape[0] % 16), (0, 0)))
            part = jnp.concatenate([held[early * rows : edges[1] * rows], lines], axis=0)
            filled = [lax.all_gather(part, "section", axis=0, tiled=False)]
        follow = layer + 1 if layer + 1 < early else None
        cur, send = apply_layer(layer, 0, follow, 8, pair_words, cur, arrived, pair_bias, mine(layer))

    ready = cur.reshape(blocks, sections // 2, half, 2 * size)
    back = jnp.zeros_like(ready[:, 0])
    for k in range(1, sections // 2):
        back = back + lax.ppermute(ready[:, k], "section", [(0, 2 * k), (1, 2 * k + 1)])
    cur = jnp.where(here < 2, ready[:, 0], back)

    cur, held = lax.optimization_barrier((cur, held))
    for first, end in zip(edges[1:], edges[2:]):
        filled.append(lax.all_gather(held[first * rows : end * rows], "section", axis=0, tiled=False))
    at = (edges[1] - early) * rows
    flat = filled[0][:, at : at + table.size // width].reshape(total, -1)
    all_bias, table = split_table(flat, blocks, size, slots, parts)
    send = jnp.take(cur, table[early, words:], axis=0)
    for layer in range(early, total):
        chunk = sum(layer >= edge for edge in edges) - 1
        follow = layer + 1 if layer + 1 < total else None
        cur, send = apply_layer(
            layer, layer - edges[chunk], follow, 16, table, cur, exchange(send), all_bias, filled[chunk]
        )
    out = cur.reshape(blocks, half, 2, size).transpose(2, 1, 0, 3)
    return out.reshape(images.shape)


def solution(mesh):
    placed = (
        P("section", None, "dom"),
        P("section", "dom", None, None),
        P("section", "dom"),
        P("section", None, None),
        P("section", "dom"),
    )
    return jax.shard_map(shards, mesh=mesh, in_specs=placed, out_specs=P("section", None, "dom"), check_vma=False)
```

```python
import jax
import jax.numpy as jnp
from jax import lax
from jax.experimental import pallas as pl
from jax.experimental.pallas import tpu as pltpu
from jax.sharding import PartitionSpec as P


def tables(bias, pattern, counts, parts, me):
    layers, columns, slots = pattern.shape
    per = columns // parts
    by_part = pattern.reshape(layers, parts, per * slots)
    wanted = jnp.max(jnp.where(by_part // per == me, by_part % per, 0), axis=2)
    own = lax.dynamic_slice_in_dim(pattern, me * per, per, 1)
    owner = own // per
    source = jnp.where(owner == me, own % per, per + owner)
    live = jnp.arange(slots)[None, None, :] < counts[:, :, None]
    source = jnp.where(live, source, per + parts)
    small = jnp.concatenate([source.reshape(layers, per * slots), wanted], axis=1)
    return jnp.concatenate([bias, small.astype(jnp.bfloat16)], axis=1)


def layer_kernel(layer, step, follow, unroll, table, cur, arrived, bias, weights, *rest):
    if follow is None:
        new, pool = rest
    else:
        new, send, pool = rest
    blocks, half, lanes = cur.shape
    parts = arrived.shape[0]
    size = lanes // 2
    slots = weights.shape[2] // size
    each = blocks // weights.shape[0]
    base = step * each * size
    low = lax.broadcasted_iota(jnp.int32, (half, lanes), 1) < size

    def spread(tile, at):
        t = tile.astype(jnp.float32)
        r = pltpu.roll(t, size, 1)
        pool[at, 0:half, :] = jnp.where(low, t, r).astype(jnp.bfloat16)
        pool[at, half : 2 * half, :] = jnp.where(low, r, t).astype(jnp.bfloat16)

    for b in range(blocks):
        spread(cur[b], b)
    for q in range(parts):
        spread(arrived[q], blocks + q)
    pool[blocks + parts] = jnp.zeros((2 * half, lanes), jnp.bfloat16)
    low2 = lax.broadcasted_iota(jnp.int32, (2 * half, lanes), 1) < size

    def column(n, carry):
        pairs = []
        for s in range(0, slots, 2):
            left = pool[table[layer, n * slots + s]]
            right = pool[table[layer, n * slots + s + 1]]
            pairs.append(jnp.where(low2, left, right))
        acc = lax.dot_general(
            jnp.concatenate(pairs, axis=1),
            weights[n // each, pl.ds(pl.multiple_of(base + n % each * size, size), size), :],
            (((1,), (1,)), ((), ())),
            preferred_element_type=jnp.float32,
        )
        tile = jnp.concatenate([acc[0:half], acc[half : 2 * half]], axis=1)
        tile = tile + bias[layer, pl.ds(n, 1), :]
        new[n] = jnp.clip(tile, 0.0, 32.0).astype(jnp.bfloat16)
        return carry

    lax.fori_loop(0, blocks, column, 0, unroll=unroll)
    if follow is not None:
        for q in range(parts):
            send[q] = new[table[follow, blocks * slots + q]]


def on_chip(x):
    return pltpu.with_memory_space_constraint(x, pltpu.VMEM)


def apply_layer(layer, step, follow, unroll, table, cur, arrived, bias, weights):
    tile = pltpu.VMEM(cur.shape, cur.dtype)
    vmem = pl.BlockSpec(memory_space=pltpu.VMEM)
    blocks, half, lanes = cur.shape
    n_out = 1 if follow is None else 2

    def body(*refs):
        layer_kernel(layer, step, follow, unroll, *refs)

    out = pl.pallas_call(
        body,
        out_shape=[tile] * n_out,
        in_specs=[pl.BlockSpec(memory_space=pltpu.SMEM), vmem, vmem, vmem, vmem],
        out_specs=[vmem] * n_out,
        scratch_shapes=[
            pltpu.VMEM((blocks + arrived.shape[0] + 1, 2 * half, lanes), jnp.bfloat16),
        ],
        compiler_params=pltpu.CompilerParams(vmem_limit_bytes=(3 + half // 16) * 1024 * 1024),
        name="layer",
    )(table, on_chip(cur), on_chip(arrived), on_chip(bias), on_chip(weights))
    return out if follow is not None else (out[0], None)


def split_table(flat, blocks, size, slots, parts):
    rows = flat.shape[0]
    bias = flat[:, : blocks * size].reshape(rows, blocks, size).astype(jnp.float32)
    words = flat[:, blocks * size : blocks * (size + slots) + parts].astype(jnp.int32)
    return jnp.concatenate([bias, bias], axis=2), words


def exchange(send):
    return lax.all_to_all(send, "dom", split_axis=0, concat_axis=0, tiled=True)


def place_kernel(here, *refs):
    count = len(refs) - 4
    pieces, held, stage, take, give = refs[:count], *refs[count:]
    sources = [lax.rem(here[0] + count - d, count) for d in range(count)]
    ins = [pltpu.make_async_copy(pieces[d], stage.at[d], take.at[d]) for d in range(count)]
    outs = [pltpu.make_async_copy(stage.at[d], held.at[sources[d]], give.at[d]) for d in range(count)]
    for copy in ins:
        copy.start()
    for copy, onward in zip(ins, outs):
        copy.wait()
        onward.start()
    for onward in outs:
        onward.wait()


def place(here, pieces):
    count = len(pieces)
    shape = (count, *pieces[0].shape)
    hbm = pl.BlockSpec(memory_space=pl.ANY)
    return pl.pallas_call(
        place_kernel,
        out_shape=jax.ShapeDtypeStruct(shape, pieces[0].dtype),
        in_specs=[pl.BlockSpec(memory_space=pltpu.SMEM)] + [hbm] * count,
        out_specs=hbm,
        scratch_shapes=[
            pltpu.VMEM(shape, pieces[0].dtype),
            pltpu.SemaphoreType.DMA((count,)),
            pltpu.SemaphoreType.DMA((count,)),
        ],
        compiler_params=pltpu.CompilerParams(vmem_limit_bytes=4 * 1024 * 1024),
        name="place",
    )(here.reshape(1), *pieces)


def shards(images, weights, bias, pattern, counts):
    parts = lax.axis_size("dom")
    sections = lax.axis_size("section")
    me = lax.axis_index("dom")
    here = lax.axis_index("section")
    own_layers, blocks, size, width = weights.shape
    slots = pattern.shape[2]
    total = own_layers * sections
    rows = blocks // sections * size
    half = images.shape[1] // 2
    words = blocks * slots
    pair = [(0, 1), (1, 0)]
    early = 2 * own_layers
    even = here % 2 == 0

    cur = images.reshape(2, half, blocks, size).transpose(2, 1, 0, 3).reshape(blocks, half, 2 * size)
    shares = [cur]
    for k in range(1, sections // 2):
        shares.append(lax.ppermute(cur, "section", [(2 * k, 0), (2 * k + 1, 1)]))
    table = tables(bias, pattern, counts, parts, me)
    table = jnp.pad(table, ((0, 0), (0, -table.shape[1] % 1024)))
    other = lax.ppermute(table, "section", pair)
    partner = []
    for k in range(own_layers):
        partner.append(lax.ppermute(weights[k], "section", pair))

    split = weights.reshape(own_layers, sections, rows, width)
    pieces = [lax.dynamic_index_in_dim(split, here, 1, keepdims=False)]
    for d in range(1, sections):
        piece = lax.dynamic_index_in_dim(split, (here + d) % sections, 1, keepdims=False)
        pairs = [(s, (s + d) % sections) for s in range(2, sections)]
        pieces.append(lax.ppermute(piece, "section", pairs))
    both = jnp.concatenate([jnp.where(even, table, other), jnp.where(even, other, table)], axis=0)
    pair_bias, pair_words = split_table(both, blocks, size, slots, parts)

    def mine(layer):
        k = layer % own_layers
        ours = even if layer < own_layers else jnp.logical_not(even)
        return jnp.where(ours, weights[k], partner[k]).reshape(1, blocks * size, width)


    cur = jnp.concatenate(shares, axis=1)
    send = jnp.take(cur, pair_words[0, words:], axis=0)
    edges = [early, 7, 11, 15, total]
    for layer in range(early):
        arrived = exchange(send)
        if layer == 1:
            arrived, pieces, partner[1] = lax.optimization_barrier((arrived, pieces, partner[1]))
            held = place(here, pieces).reshape(total * rows, width)
            lines = table.reshape(-1, width)
            lines = jnp.pad(lines, ((0, -lines.shape[0] % 16), (0, 0)))
            part = jnp.concatenate([held[early * rows : edges[1] * rows], lines], axis=0)
            filled = [lax.all_gather(part, "section", axis=0, tiled=False)]
            parted = [held[first * rows : end * rows] for first, end in zip(edges[1:], edges[2:])]
        follow = layer + 1 if layer + 1 < early else None
        cur, send = apply_layer(layer, 0, follow, 8, pair_words, cur, arrived, pair_bias, mine(layer))

    ready = cur.reshape(blocks, sections // 2, half, 2 * size)
    back = jnp.zeros_like(ready[:, 0])
    for k in range(1, sections // 2):
        back = back + lax.ppermute(ready[:, k], "section", [(0, 2 * k), (1, 2 * k + 1)])
    cur = jnp.where(here < 2, ready[:, 0], back)

    cur, parted = lax.optimization_barrier((cur, parted))
    filled += [lax.all_gather(part, "section", axis=0, tiled=False) for part in parted]
    at = (edges[1] - early) * rows
    flat = filled[0][:, at : at + table.size // width].reshape(total, -1)
    all_bias, table = split_table(flat, blocks, size, slots, parts)
    send = jnp.take(cur, table[early, words:], axis=0)
    for layer in range(early, total):
        chunk = sum(layer >= edge for edge in edges) - 1
        follow = layer + 1 if layer + 1 < total else None
        cur, send = apply_layer(
            layer, layer - edges[chunk], follow, 16, table, cur, exchange(send), all_bias, filled[chunk]
        )
    out = cur.reshape(blocks, half, 2, size).transpose(2, 1, 0, 3)
    return out.reshape(images.shape)


def solution(mesh):
    placed = (
        P("section", None, "dom"),
        P("section", "dom", None, None),
        P("section", "dom"),
        P("section", None, None),
        P("section", "dom"),
    )
    return jax.shard_map(shards, mesh=mesh, in_specs=placed, out_specs=P("section", None, "dom"), check_vma=False)
```
